32 devices in a mesh: expert: 4 (over z), tensor: 8 (over y, x, core).
Axes of the slice: x: 2, y: 2, z: 4, core: 2. Of those that a mesh axis runs over, the one named last changes fastest.
Arguments:
- tokens: bfloat16 [1024, 4096], P(('expert', 'tensor')), may hold values from -6 to 6
- router: float32 [4096, 4], replicated, may hold values from -0.09375 to 0.09375
- choice_ids: int32 [1024, 2], P(('expert', 'tensor')), may hold values from 0 to 3, all different within a row; in each aligned block of 32 rows (0 to 31, 32 to 63, ...) at most 20 rows name the same one
- w_gate: bfloat16 [4, 4096, 14336], P('expert', None, 'tensor'), may hold values from -0.09375 to 0.09375
- w_up: bfloat16 [4, 4096, 14336], P('expert', None, 'tensor'), may hold values from -0.09375 to 0.09375
- w_down: bfloat16 [4, 14336, 4096], P('expert', 'tensor'), may hold values from -0.046875 to 0.046875
Outputs:
- mixed: bfloat16 [1024, 4096], P(('expert', 'tensor'))
The draws below stay inside these ranges and needn't reach their ends.
Inputs may be any that keep to these rules, and one draw needn't show every extreme that they name: `choice_ids`: the 2 experts of a token differ. In each aligned block of 32 rows (the rows of one device) each expert is named by at most 20 rows, a bound that some block reaches.
All inputs are finite; a program needn't handle non-finite values.
Results may differ from the reference program's by a relative error of at most 0.015.
Values may be sent and summed in bfloat16 or wider, within the bound.
No kernel may reach another device: no remote copies, remote signals or barrier semaphores. Data moves between devices by JAX's collectives and lax.ppermute only.
A program may use at most 128 MiB of HBM per device.

```python
import math
import jax
import jax.numpy as jnp
import numpy as np
from jax import lax

D = 4096
FF = 14336
TOP = 2
TOK_DEV = 32
EXPERTS = 4
TOKENS = 1024
CAP = 20
N_EXPERT = 4
N_TENSOR = 8


def levels(rng, shape, cuts, smallest, largest):
    level = 1.0
    for position, parts in cuts:
        steps = jax.random.uniform(jax.random.fold_in(jax.random.fold_in(rng, 6), position), (parts,), jnp.float32, smallest / len(cuts), largest / len(cuts))
        level = level * jnp.repeat(jnp.exp(steps), shape[position] // parts).reshape((-1,) + (1,) * (len(shape) - 1 - position))
    return level


def shared_out(stream_key, own, number, rows, number_of, top, reach, slope):
    order = jax.random.permutation(stream_key, number_of)
    heavy_load, ordinary = shares(number_of, rows * top, reach, slope, True), shares(number_of, rows * top, reach, slope, False)
    places = jnp.arange(number_of)

    def named(tallies, offset_by):
        used = int((tallies > 0).sum())
        fixed = max(1, used // 4)
        moved = fixed + (places - fixed + offset_by * (used - fixed)) % max(1, number_of - fixed)
        return jnp.zeros((number_of,), jnp.int32).at[order[jnp.where(places < fixed, places, moved)]].set(jnp.asarray(tallies, jnp.int32))

    tallies = jnp.where(number % 4 == 0, named(heavy_load, number // 4), named(ordinary, number - number // 4 - 1))
    mixed = jax.random.permutation(jax.random.fold_in(own, 3), number_of)
    source_of, receiver = mixed[0:number_of // 2 * 2:2], mixed[1:number_of // 2 * 2:2]
    margin = jnp.minimum(tallies[source_of] - 1, reach - tallies[receiver]) // 2
    margin = jnp.where((source_of == order[0]) | (receiver == order[0]) | (tallies[receiver] == 0), 0, jnp.maximum(margin, 0))
    moved = jax.random.randint(jax.random.fold_in(own, 4), (number_of // 2,), 0, 1 << 20) % (margin + 1)
    tallies = tallies.at[source_of].add(-moved).at[receiver].add(moved)
    items = jnp.searchsorted(jnp.cumsum(tallies), jnp.arange(rows * top), side="right").astype(jnp.int32)
    listing = items.reshape(top, rows).T
    listing = listing[jax.random.permutation(jax.random.fold_in(own, 1), rows)]
    offset_by = jax.random.randint(jax.random.fold_in(own, 2), (rows, 1), 0, top)
    return jnp.take_along_axis(listing, (jnp.arange(top)[None, :] + offset_by) % top, axis=1)


def shares(number_of, total, limit, slope, full):
    portions = [(1 << 20) // math.isqrt(grade ** slope) + 1 for grade in range(1, number_of + 1)]
    largest = limit if full else min(limit, max(-(-total // number_of), total * portions[0] // sum(portions)))
    least = 1 if total - largest >= number_of - 1 else 0
    given, surplus = [largest] + [least] * (number_of - 1), total - largest - least * (number_of - 1)
    while surplus > 0:
        free = [i for i in range(1, number_of) if given[i] < largest] or [i for i in range(1, number_of) if given[i] < limit]
        whole, left = sum([portions[i] for i in free]), surplus
        for i in free:
            extra = min(limit - given[i], max(1, left * portions[i] // whole), surplus)
            given[i] = given[i] + extra
            surplus = surplus - extra
    return np.array(given)


def bell_draw(rng, extent, deviation, most, cuts=(), kind=jnp.bfloat16):
    values = jax.random.normal(rng, extent, jnp.float32) * deviation
    if len(cuts) > 0:
        values = levels(rng, extent, cuts, -0.22, 0.18) * values
    return jnp.clip(values, min=-most, max=most).astype(kind)


def setup_inputs(seed: int = 0) -> dict:
    splits = jax.random.split(jax.random.key(seed), 7)
    tokens = bell_draw(splits[0], (TOKENS, D), 1.0, 6.0, ((0, 32),))
    router = bell_draw(splits[1], (D, EXPERTS), D ** -0.5, 0.09375, (), jnp.float32)
    choice_ids_keys = jax.random.split(jax.random.fold_in(splits[2], 1), TOKENS // TOK_DEV)
    choice_ids_turns = jax.random.permutation(jax.random.fold_in(splits[2], 3), TOKENS // TOK_DEV)
    choice_ids = jax.vmap(lambda own, number: shared_out(jax.random.fold_in(splits[2], 2), own, number, TOK_DEV, EXPERTS, TOP, CAP, 2))(choice_ids_keys, choice_ids_turns).reshape((TOKENS, TOP))
    w_gate = bell_draw(splits[3], (EXPERTS, D, FF), D ** -0.5, 0.09375, ((0, 4), (2, 8)))
    w_up = bell_draw(splits[4], (EXPERTS, D, FF), D ** -0.5, 0.09375, ((0, 4), (2, 8)))
    w_down = bell_draw(splits[5], (EXPERTS, FF, D), FF ** -0.5, 0.046875, ((0, 4), (1, 8)))
    return dict(tokens=tokens, router=router, choice_ids=choice_ids, w_gate=w_gate, w_up=w_up, w_down=w_down)


def expert_block(expert_rows, weight_gate, weight_up, weight_down):
    gate_proj = jnp.dot(expert_rows, weight_gate, preferred_element_type=jnp.float32)
    up_proj = jnp.dot(expert_rows, weight_up, preferred_element_type=jnp.float32)
    hidden = (jax.nn.silu(gate_proj) * up_proj).astype(jnp.bfloat16)
    row_total = hidden.shape[0]
    hidden_width = FF // N_TENSOR
    shards = hidden.reshape(row_total, N_TENSOR, hidden_width).transpose(1, 0, 2)
    down_shards = weight_down.reshape(N_TENSOR, hidden_width, D)

    def accumulate(running, operand):
        partial_value = jnp.dot(operand[0], operand[1], preferred_element_type=jnp.float32)
        rounded = lax.optimization_barrier(partial_value.astype(jnp.bfloat16))
        return running + rounded.astype(jnp.float32), None

    running, _ = lax.scan(accumulate, jnp.zeros((row_total, D), jnp.float32), (shards, down_shards))
    return running.astype(jnp.bfloat16)


def reference(tokens, router, choice_ids, w_gate, w_up, w_down):
    sources = N_EXPERT * N_TENSOR
    logits = jnp.dot(tokens.astype(jnp.float32), router, precision=lax.Precision.HIGHEST)
    picked = jnp.take_along_axis(logits, choice_ids, axis=1)
    gate_weights = jax.nn.softmax(picked, axis=1)
    flat_ids = choice_ids.reshape(sources, TOK_DEV * TOP)
    onehot = (flat_ids[:, :, None] == jnp.arange(EXPERTS, dtype=jnp.int32)[None, None, :]).astype(jnp.int32)
    slot_rank = jnp.cumsum(onehot, axis=1) - onehot
    slot_index = jnp.sum(slot_rank * onehot, axis=2)
    source_ids = jnp.arange(sources, dtype=jnp.int32)[:, None]
    destination = ((flat_ids * sources + source_ids) * CAP + slot_index).reshape(-1).astype(jnp.int32)
    total_rows = EXPERTS * sources * CAP
    token_of = (jnp.arange(TOKENS * TOP, dtype=jnp.int32) // TOP).astype(jnp.int32)
    row_token = jnp.zeros((total_rows,), jnp.int32).at[destination].set(token_of)
    row_valid = jnp.zeros((total_rows,), tokens.dtype).at[destination].set(1)
    gathered = (tokens[row_token] * row_valid[:, None]).reshape(EXPERTS, sources * CAP, D)
    outputs = lax.map(lambda items: expert_block(items[0], items[1], items[2], items[3]), (gathered, w_gate, w_up, w_down))
    flat_out = outputs.reshape(total_rows, D)[destination].astype(jnp.float32).reshape(TOKENS, TOP, D)
    result = jnp.sum(flat_out * gate_weights[:, :, None], axis=1)
    return result.astype(jnp.bfloat16)
```

```python
import jax
import jax.numpy as jnp
from jax import lax
from jax.sharding import PartitionSpec as P

CHUNKS = 2


def swap(value, axis, size, bit):
    return lax.ppermute(value, axis, [(i, i ^ bit) for i in range(size)])


def shift(value, axis, size, step):
    return lax.ppermute(value, axis, [(i, (i + step) % size) for i in range(size)])


def lane_orders(size):
    bits = [1 << b for b in range(size.bit_length() - 1)]
    return [bits[1:], bits[1:][::-1]], bits[0]


def gather_lane(piece, size, order):
    pieces = {0: piece}
    rows = piece.shape[0]
    for bit in order:
        keys = sorted(pieces)
        sent = jnp.concatenate([pieces[key] for key in keys], 0) if len(keys) > 1 else pieces[keys[0]]
        came = swap(sent, "tensor", size, bit)
        for place, key in enumerate(keys):
            pieces[key ^ bit] = came[place * rows : (place + 1) * rows]
    return jnp.concatenate([pieces[key] for key in sorted(pieces)], 0)


def scatter_lane(pieces, size, order):
    for bit in reversed(order):
        kept = sorted(key for key in pieces if not key & bit)
        rows = pieces[kept[0]].shape[0]
        sent = jnp.concatenate([pieces[key ^ bit] for key in kept], 0)
        came = swap(sent, "tensor", size, bit)
        pieces = {
            key: (
                pieces[key].astype(jnp.float32)
                + came[place * rows : (place + 1) * rows].astype(jnp.float32)
            ).astype(jnp.bfloat16)
            for place, key in enumerate(kept)
        }
    return pieces[0]


def gather_rows(rows, size):
    orders, last = lane_orders(size)
    width = rows.shape[1] // len(orders)
    lanes = [
        gather_lane(rows[:, lane * width : (lane + 1) * width], size, order)
        for lane, order in enumerate(orders)
    ]
    mine = jnp.concatenate(lanes, 1)
    return jnp.concatenate([mine, swap(mine, "tensor", size, last)], 0)


def scatter_rows(partial_value, size):
    orders, last = lane_orders(size)
    half = partial_value.shape[0] // 2
    came = swap(partial_value[half:], "tensor", size, last)
    total = (partial_value[:half].astype(jnp.float32) + came.astype(jnp.float32)).astype(
        jnp.bfloat16
    )
    width = total.shape[1] // len(orders)
    count = size // 2
    rows = half // count
    lanes = []
    for lane, order in enumerate(orders):
        columns = total[:, lane * width : (lane + 1) * width]
        pieces = {
            2 * place: columns[place * rows : (place + 1) * rows] for place in range(count)
        }
        lanes.append(scatter_lane(pieces, size, order))
    return jnp.concatenate(lanes, 1)


def expert_rows(rows, weight_gate, weight_up, weight_down):
    gate_proj = jnp.dot(rows, weight_gate, preferred_element_type=jnp.float32)
    up_proj = jnp.dot(rows, weight_up, preferred_element_type=jnp.float32)
    hidden = (jax.nn.silu(gate_proj) * up_proj).astype(jnp.bfloat16)
    return jnp.dot(hidden, weight_down, preferred_element_type=jnp.float32).astype(jnp.bfloat16)


def on_device(tokens, router, choice_ids, w_gate, w_up, w_down):
    tok_count = tokens.shape[0]
    top_count = choice_ids.shape[1]
    experts = lax.axis_size("expert")
    size = lax.axis_size("tensor")
    capacity = tok_count * top_count * 5 // (experts * 4)
    group_rows = experts * capacity
    plane = lax.axis_index("expert")

    flat_ids = choice_ids.reshape(-1)
    onehot = (flat_ids[:, None] == jnp.arange(experts, dtype=jnp.int32)[None, :]).astype(jnp.int32)
    slot_rank = jnp.cumsum(onehot, axis=0) - onehot
    slot_index = jnp.sum(slot_rank * onehot, axis=1)
    relative = jnp.mod(flat_ids - plane, experts)
    destination = (relative * capacity + slot_index).reshape(tok_count, top_count)
    named = jnp.arange(group_rows, dtype=jnp.int32)[:, None, None] == destination[None]
    dispatch_map = jnp.any(named, axis=2).astype(jnp.bfloat16)
    buffer = jnp.dot(dispatch_map, tokens, preferred_element_type=jnp.float32).astype(jnp.bfloat16)

    arrived = [
        buffer[:capacity]
        if step == 0
        else shift(buffer[step * capacity : (step + 1) * capacity], "expert", experts, step)
        for step in range(experts)
    ]
    per_chunk = experts // CHUNKS
    returned = []
    for chunk in range(CHUNKS):
        rows = jnp.concatenate(arrived[chunk * per_chunk : (chunk + 1) * per_chunk], 0)
        partial_value = expert_rows(gather_rows(rows, size), w_gate[0], w_up[0], w_down[0])
        own = scatter_rows(partial_value, size)
        for place in range(per_chunk):
            step = chunk * per_chunk + place
            piece = own[place * capacity : (place + 1) * capacity]
            returned.append(piece if step == 0 else shift(piece, "expert", experts, -step))
    returned = jnp.concatenate(returned, 0)

    logits = jnp.dot(tokens.astype(jnp.float32), router, precision=lax.Precision.HIGHEST)
    picked = jnp.take_along_axis(logits, choice_ids, axis=1)
    gate_weights = jax.nn.softmax(picked, axis=1)
    result = 0.0
    for k in range(top_count):
        chosen = (
            destination[:, k][:, None] == jnp.arange(group_rows, dtype=jnp.int32)[None, :]
        ).astype(jnp.bfloat16)
        taken = jnp.dot(chosen, returned, preferred_element_type=jnp.float32)
        result = result + taken * gate_weights[:, k][:, None]
    return result.astype(jnp.bfloat16)


def solution(mesh):
    in_specs = (
        P(("expert", "tensor"), None),
        P(),
        P(("expert", "tensor"), None),
        P("expert", None, "tensor"),
        P("expert", None, "tensor"),
        P("expert", "tensor", None),
    )
    out_specs = P(("expert", "tensor"), None)
    return jax.shard_map(
        on_device, mesh=mesh, in_specs=in_specs, out_specs=out_specs, check_vma=False
    )
```
